32 devices in a mesh: vocab: 8 (over y, x, core), hid: 4 (over z).
Axes of the slice: x: 2, y: 2, z: 4, core: 2. Of those that a mesh axis runs over, the one named last changes fastest.
Arguments:
- hidden: bfloat16 [1, 1024, 3584], P(None, 'vocab', 'hid'), may hold values from -30 to 30
- unembed: bfloat16 [3584, 81920], P(None, ('vocab', 'hid')), may hold values from -10 to 10
- labels: int32 [1024], P('vocab'), may hold values from 0 to 81919
Outputs:
- token_loss: float32 [1, 1024], replicated
- layer_loss: float32 [1], replicated
The draws below stay inside these ranges and needn't reach their ends.
All inputs are finite; a program needn't handle non-finite values.
Results may differ from the reference program's by a relative error of at most 0.0003.
Values may be sent and summed in bfloat16 or wider, within the bound.
A program may use at most 128 MiB of HBM per device.

```python
import math
import jax
import jax.numpy as jnp
import numpy as np
from jax import lax

D = 3584
V = 81920
LAYERS = 1
TOK_DEV = 128
TOKENS = 1024


def draw_hidden(key, part):
    values = jnp.clip(jax.random.normal(jax.random.fold_in(key, 1), (LAYERS, TOKENS, D), jnp.float32), -6.0, 6.0)
    return values.astype(jnp.bfloat16)


def draw_unembed(key, part):
    values = jnp.clip(jax.random.normal(jax.random.fold_in(key, 3), (D, V), jnp.float32), -6.0, 6.0)
    values = values * (3.0 / math.sqrt(D))
    return values.astype(jnp.bfloat16)


def set_ends(result, key, smallest, top_value):
    index_at = [jax.random.randint(jax.random.fold_in(key, axis), (), 0, length) for axis, length in enumerate(result.shape)]
    widest = result.shape.index(max(result.shape))
    next_to = index_at[:widest] + [(index_at[widest] + 1) % result.shape[widest]] + index_at[widest + 1:]
    return result.at[tuple(index_at)].set(smallest).at[tuple(next_to)].set(top_value)


def wide_ids(own_key, shape, number_of, skew):
    loads = [min(1 << octave, number_of + 1 - (1 << octave)) * (1 << 20) // math.isqrt((1 << octave) ** skew) + 1 for octave in range((number_of + 1).bit_length()) if 1 << octave <= number_of]
    scale = 1 + sum(loads) // (1 << 30)
    grid = np.cumsum(np.array([max(1, weight // scale) for weight in loads]))
    pick = jax.random.randint(jax.random.fold_in(own_key, 1), shape, 0, int(grid[len(loads) - 1]))
    start = jnp.left_shift(1, jnp.searchsorted(jnp.asarray(grid, jnp.int32), pick, side="right").astype(jnp.int32))
    rank = start - 1 + jax.random.randint(jax.random.fold_in(own_key, 4), shape, 0, 1 << 30) % jnp.minimum(start, number_of + 1 - start)
    return jax.random.permutation(jax.random.fold_in(own_key, 2), number_of)[rank].astype(jnp.int32)


def setup_inputs(seed: int = 0) -> dict:
    splits = jax.random.split(jax.random.key(seed), 4)
    hidden = draw_hidden(jax.random.fold_in(splits[3], 71), 0)
    unembed = draw_unembed(jax.random.fold_in(splits[3], 71), 0)
    labels = set_ends(wide_ids(splits[2], (TOKENS,), V, 2), jax.random.fold_in(splits[2], 3), 0, V - 1).astype(jnp.int32)
    return dict(hidden=hidden, unembed=unembed, labels=labels)


def reference(hidden, unembed, labels):
    token_rows = hidden.reshape(-1, TOK_DEV, D)
    targets = jnp.tile(labels, LAYERS).reshape(-1, TOK_DEV).astype(jnp.int32)

    def one_block(block_pair):
        row_block, wanted = block_pair
        logits = jnp.dot(row_block, unembed, preferred_element_type=jnp.float32)
        row_peak = jnp.max(logits, axis=-1)
        row_total = jnp.sum(jnp.exp(logits - row_peak[:, None]), axis=-1)
        picked = jnp.take_along_axis(logits, wanted[:, None], axis=-1)[:, 0]
        return row_peak + jnp.log(row_total) - picked

    token_loss = lax.map(one_block, (token_rows, targets)).reshape(LAYERS, TOKENS)
    return token_loss, jnp.mean(token_loss, axis=1)
```

```python
import functools

import jax
import jax.numpy as jnp
from jax import lax
from jax.experimental import pallas as pl
from jax.experimental.pallas import tpu as pltpu
from jax.sharding import PartitionSpec as P

MESH = pl.DeviceIdType.MESH
LANES = 128
CUTS = 2
TILE = 2560
ORDER = (
    (0, 2, 0, 1), (0, 1, 0, 0), (0, 0, 1, 0), (0, 0, 1, 1), (0, 1, 0, 1), (0, 2, 0, 0),
    (2, 0, 0, 0), (1, 0, 1, 0), (1, 1, 0, 0), (1, 1, 0, 1), (1, 0, 1, 1), (1, 2, 0, 1),
    (1, 2, 0, 0), (2, 1, 0, 0), (1, 1, 1, 0), (1, 2, 1, 0), (2, 0, 1, 0), (1, 0, 2, 0),
    (1, 1, 1, 1), (1, 2, 1, 1), (2, 2, 0, 0), (1, 0, 2, 1), (2, 1, 1, 0), (1, 3, 1, 0),
    (1, 3, 0, 1), (2, 0, 2, 0), (1, 2, 2, 0), (1, 3, 0, 0), (2, 2, 1, 0), (1, 3, 1, 1),
    (1, 0, 3, 0), (1, 0, 3, 1), (1, 1, 2, 0), (2, 3, 0, 0), (1, 3, 2, 0), (1, 1, 2, 1),
    (1, 2, 2, 1), (2, 3, 1, 0), (1, 3, 2, 1), (2, 1, 2, 0), (2, 2, 2, 0), (2, 0, 3, 0),
    (1, 3, 3, 0), (1, 1, 3, 1), (1, 2, 3, 0), (1, 1, 3, 0), (1, 3, 3, 1), (1, 2, 3, 1),
    (2, 2, 3, 0), (2, 1, 3, 0), (2, 3, 2, 0), (2, 3, 3, 0),
)


def bits_of(mask):
    return [1 << b for b in range(mask.bit_length()) if mask >> b & 1]


def parent(group, slab):
    dims = bits_of(group)
    if group == 0:
        return (0, slab - 1), ("hid", 1)
    if len(dims) == 1:
        return (0, slab), ("vocab", group)
    if slab < len(dims):
        return (group ^ dims[slab], slab), ("vocab", dims[slab])
    return (group, slab - 1), ("hid", 1)


def depth_of(group, slab):
    return 0 if (group, slab) == (0, 0) else 1 + depth_of(*parent(group, slab)[0])


def plan(n_g, n_h, cuts):
    blocks = [(g, j) for j in range(n_h) for g in range(n_g) if (g, j) != (0, 0)]
    direct = [b for b in blocks if parent(*b)[0] == (0, 0)]
    ops = [("s", b, c) for c in range(cuts) for b in direct]
    arrived = {(0, 0)}
    done = set()

    def compute():
        for j in range(n_h):
            for g in range(n_g):
                need = {(g, j), (g, j - j % 2)}
                if (g, j) not in done and need <= arrived:
                    done.add((g, j))
                    ops.append(("c", g, j))

    compute()
    for b in sorted(blocks, key=lambda b: (depth_of(*b), b[1], b[0])):
        ops.extend(("w", b, c) for c in range(cuts))
        arrived.add(b)
        compute()
    return ops


def flip(index, mask):
    for bit in bits_of(mask):
        index = index + bit - 2 * bit * lax.rem(index // bit, 2)
    return index


def combine(parts, blocks):
    sums = [part[0:blocks] for part in parts]
    top = functools.reduce(jnp.maximum, sums)
    total = sum(jnp.exp(own - top) for own in sums)
    return top + jnp.log(total), sum(part[blocks : 2 * blocks] for part in parts)


def kernel(
    n_v, n_h, layers,
    hid_hbm, w_hbm, lab_ref,
    loss_ref, mean_ref,
    buf, w, acc, labs, lanes, rel_stats, line, plane,
    own_sem, w_sem, send_sem, recv_sem, lab_send, lab_recv, line_send, line_recv, plane_send, plane_recv,
):
    v, z = lax.axis_index("vocab"), lax.axis_index("hid")
    rows = hid_hbm.shape[0]
    depth = hid_hbm.shape[1]
    cols = w_hbm.shape[1]
    first_col = (v * n_h + z) * cols
    dims = [1 << b for b in range((n_v // 2).bit_length() - 1)]
    groups = sorted(range(n_v // 2), key=lambda g: (len(bits_of(g)), g))
    pos = {2 * g + c: 2 * i + c for i, g in enumerate(groups) for c in range(2)}
    blocks = n_v * layers

    own = pltpu.make_async_copy(hid_hbm, buf.at[pl.ds(0, rows), pl.ds(0, depth)], own_sem)
    own.start()
    w_copies = []
    for s in range(n_h):
        src = lax.rem(z - s + n_h, n_h)
        copy = pltpu.make_async_copy(
            w_hbm.at[pl.ds(pl.multiple_of(src * depth, depth), depth)], w.at[pl.ds(s * depth, depth)], w_sem.at[s]
        )
        w_copies.append(copy)

    barrier = pltpu.get_barrier_semaphore()
    line_peers = [lax.rem(z + j, n_h) for j in range(1, n_h)]
    for peer in line_peers:
        pl.semaphore_signal(barrier, inc=1, device_id=(v, peer), device_id_type=MESH)
    for m in range(1, n_v):
        pl.semaphore_signal(barrier, inc=1, device_id=(flip(v, m), z), device_id_type=MESH)
    for copy in w_copies:
        copy.start()
    pl.semaphore_wait(barrier, n_h + n_v - 2)
    own.wait()

    cuts = CUTS if n_v * n_h <= 64 else 1
    piece = rows // cuts
    sends = []

    groups_at = {g: i for i, g in enumerate(groups)}
    children = {}
    for g in range(n_v // 2):
        for s in range(n_h):
            if (g, s) != (0, 0):
                source, hop = parent(g, s)
                children.setdefault(source, []).append(((g, s), hop))

    def block_copy(m, s, to_m, to_s, cut, device):
        k = min(len(sends), send_sem.shape[0] - 1)
        return pltpu.make_async_remote_copy(
            src_ref=buf.at[pl.ds(pos[m] * rows + cut * piece, piece), pl.ds(s * depth, depth)],
            dst_ref=buf.at[pl.ds(pos[to_m] * rows + cut * piece, piece), pl.ds(to_s * depth, depth)],
            send_sem=send_sem.at[k],
            recv_sem=recv_sem.at[(to_m * n_h + to_s) * cuts + cut],
            device_id=device, device_id_type=MESH,
        )

    def send(m, s, to_m, to_s, cut, device):
        copy = block_copy(m, s, to_m, to_s, cut, device)
        copy.start()
        sends.append(copy)

    def wait_block(m, s, cut):
        block_copy(m, s, m, s, cut, (flip(v, 1), z)).wait_recv()

    def hand_on(g, s, to, hop, cut):
        axis, mask = hop
        device = (v, lax.rem(z + mask, n_h)) if axis == "hid" else (flip(v, 2 * mask), z)
        send(2 * g, s, 2 * to[0], to[1], cut, device)

    def arrive(g, s, cut):
        wait_block(2 * g, s, cut)
        for to, hop in children.get((g, s), []):
            hand_on(g, s, to, hop, cut)
        send(2 * g, s, 2 * g + 1, s, cut, (flip(v, 1), z))

    tile = max(t for t in range(LANES, TILE + 1, LANES) if cols % t == 0)
    tiles = cols // tile
    waited = set()
    steps = {}

    def multiply(units):
        for g, s in units:
            for t in range(s - s % 2, s + 1):
                for cut in range(cuts):
                    if (g, t, cut) not in waited:
                        waited.add((g, t, cut))
                        wait_block(2 * g + 1, t, cut) if (g, t) != (0, 0) else wait_block(1, 0, cut)
                if t not in waited:
                    w_copies[t].wait()
                    waited.add(t)
        work = []
        for g, s in sorted(units, key=lambda unit: (unit[1], groups_at[unit[0]])):
            k_lo = s * depth // 256 * 256
            k_hi = (s + 1) * depth // 256 * 256 if s + 1 < n_h else n_h * depth
            first = g not in steps
            steps[g] = steps.get(g, 0) + 1
            work.append((groups_at[g], 1, k_lo, k_hi, first, steps[g] == n_h))
        jobs = []
        for at, count, k_lo, k_hi, first, last in work:
            for i, job in enumerate(jobs):
                if job[:2] == (at, count) and job[3] == k_lo and not job[5]:
                    jobs[i] = (at, count, job[2], k_hi, job[4], last)
                    break
            else:
                jobs.append((at, count, k_lo, k_hi, first, last))
        merged = []
        for job in jobs:
            if merged and merged[-1][0] + merged[-1][1] == job[0] and merged[-1][2:] == job[2:]:
                merged[-1] = (merged[-1][0], merged[-1][1] + job[1], *job[2:])
            else:
                merged.append(job)

        @pl.loop(0, tiles)
        def _(n):
            at = pl.ds(pl.multiple_of(n * tile, tile), tile)
            for row, count, k_lo, k_hi, first, last in merged:
                here = slice(row * 2 * rows, (row + count) * 2 * rows)
                value = jnp.dot(buf[here, k_lo:k_hi], w[k_lo:k_hi, at], preferred_element_type=jnp.float32)
                if not first:
                    value = acc[here, at] + value
                if not last:
                    acc[here, at] = value
                    continue
                chunks = [value[:, c : c + LANES] for c in range(0, tile, LANES)]
                old = lanes[0, here, :]
                peak = functools.reduce(jnp.maximum, chunks, old)
                total = lanes[1, here, :] * jnp.exp(old - peak)
                picked = lanes[2, here, :]
                wanted = lanes[3, here, :] - (n * tile).astype(jnp.float32)
                for i, x in enumerate(chunks):
                    total = total + jnp.exp(x - peak)
                    picked = picked + jnp.where(wanted == float(i * LANES), x, 0.0)
                lanes[0, here, :] = peak
                lanes[1, here, :] = total
                lanes[2, here, :] = picked

    def prepare():
        for copy in lab_copies:
            copy.wait()
        lane = (lax.broadcasted_iota(jnp.int32, (LANES, LANES), 1) + first_col).astype(jnp.float32)

        @pl.loop(0, blocks)
        def _(p):
            at = pl.ds(pl.multiple_of(p * LANES, LANES), LANES)
            label = jnp.broadcast_to(labs[p // layers].astype(jnp.float32), (LANES, LANES))
            lanes[0, at, :] = jnp.full((LANES, LANES), -jnp.inf, jnp.float32)
            lanes[1, at, :] = jnp.zeros((LANES, LANES), jnp.float32)
            lanes[2, at, :] = jnp.zeros((LANES, LANES), jnp.float32)
            lanes[3, at, :] = jnp.transpose(label) - lane

    def stats(first, count):
        @pl.loop(first * 2 * layers, (first + count) * 2 * layers)
        def _(p):
            at = pl.ds(pl.multiple_of(p * LANES, LANES), LANES)
            peak = jnp.transpose(lanes[0, at, :])
            row_peak = jnp.max(peak, axis=0, keepdims=True)
            total = jnp.transpose(lanes[1, at, :]) * jnp.exp(peak - row_peak)
            rel_stats[0, p] = row_peak + jnp.log(jnp.sum(total, axis=0, keepdims=True))
            rel_stats[1, p] = jnp.sum(jnp.transpose(lanes[2, at, :]), axis=0, keepdims=True)

    lab_copies = []
    for m in range(1, n_v):
        copy = pltpu.make_async_remote_copy(
            src_ref=lab_ref, dst_ref=labs.at[pos[m]],
            send_sem=lab_send.at[m - 1], recv_sem=lab_recv.at[m - 1],
            device_id=(flip(v, m), z), device_id_type=MESH,
        )
        copy.start()
        lab_copies.append(copy)
    labs[0] = lab_ref[...]

    ops = plan(n_v // 2, n_h, cuts)
    tuned = [("c", g, s) if kind == 2 else ("sw"[kind], (g, s), cut) for kind, g, s, cut in ORDER]
    if sorted(map(str, ops)) == sorted(map(str, tuned)):
        ops = tuned
    begin = 0
    while ops[begin][0] == "s":
        begin += 1
    for _, (g, s), cut in ops[:begin]:
        hand_on(0, 0, (g, s), parent(g, s)[1], cut)
    for cut in range(cuts):
        send(0, 0, 1, 0, cut, (flip(v, 1), z))
    units, prepared = [], []
    for op in ops[begin:] + [None]:
        if op is not None and op[0] == "c":
            units.append(op[1:])
            continue
        if units:
            if not prepared and any(steps.get(g, 0) + sum(u[0] == g for u in units) == n_h for g, _ in units):
                prepare()
                prepared.append(True)
            multiply(units)
            units = []
        if op is None:
            break
        if op[0] == "s":
            hand_on(0, 0, op[1], parent(*op[1])[1], op[2])
        else:
            arrive(*op[1], op[2])
    stats(0, len(groups))

    for m in range(n_v):
        for l in range(layers):
            for k in range(2):
                line[z, pl.ds(k * blocks + flip(v, m) * layers + l, 1), :] = rel_stats[k, pos[m] * layers + l]
    line_copies = []
    for j, peer in enumerate(line_peers):
        copy = pltpu.make_async_remote_copy(
            src_ref=line.at[z], dst_ref=line.at[z],
            send_sem=line_send.at[j], recv_sem=line_recv.at[j],
            device_id=(v, peer), device_id_type=MESH,
        )
        copy.start()
        line_copies.append(copy)
    for copy in line_copies:
        copy.wait_recv()
    whole, picked = combine([line[h] for h in range(n_h)], blocks)
    plane[v, 0:blocks, :] = whole
    plane[v, blocks : 2 * blocks, :] = picked
    plane_copies = []
    for m in range(1, n_v):
        copy = pltpu.make_async_remote_copy(
            src_ref=plane.at[v], dst_ref=plane.at[v],
            send_sem=plane_send.at[m - 1], recv_sem=plane_recv.at[m - 1],
            device_id=(flip(v, m), z), device_id_type=MESH,
        )
        copy.start()
        plane_copies.append(copy)
    for copy in sends + line_copies:
        copy.wait_send()
    for copy in plane_copies:
        copy.wait_recv()
    whole, picked = combine([plane[u] for u in range(n_v)], blocks)
    loss = whole - picked
    for l in range(layers):
        sums = jnp.zeros((1, LANES), jnp.float32)
        for u in range(n_v):
            row = loss[u * layers + l : u * layers + l + 1]
            loss_ref[l : l + 1, u * LANES : (u + 1) * LANES] = row
            sums = sums + row
        mean_ref[l] = jnp.sum(sums) / (n_v * LANES)
    for copy in plane_copies:
        copy.wait_send()


def body(hidden, unembed, labels, n_v, n_h):
    layers, tokens, depth = hidden.shape
    cols = unembed.shape[1]
    rows = layers * tokens
    blocks = n_v * layers
    dma = pltpu.SemaphoreType.DMA
    any_space = pl.BlockSpec(memory_space=pl.ANY)
    vmem = pl.BlockSpec(memory_space=pltpu.VMEM)
    cuts = CUTS if n_v * n_h <= 64 else 1
    return pl.pallas_call(
        functools.partial(kernel, n_v, n_h, layers),
        out_shape=(
            jax.ShapeDtypeStruct((layers, n_v * tokens), jnp.float32),
            jax.ShapeDtypeStruct((layers,), jnp.float32),
        ),
        in_specs=[any_space, any_space, vmem],
        out_specs=(vmem, pl.BlockSpec(memory_space=pltpu.SMEM)),
        scratch_shapes=[
            pltpu.VMEM((n_v * rows, n_h * depth), jnp.bfloat16),
            pltpu.VMEM((n_h * depth, cols), jnp.bfloat16),
            pltpu.VMEM((n_v * rows, cols), jnp.float32),
            pltpu.VMEM((n_v, 1, tokens), jnp.int32),
            pltpu.VMEM((4, n_v * rows, LANES), jnp.float32),
            pltpu.VMEM((2, blocks, 1, tokens), jnp.float32),
            pltpu.VMEM((n_h, 2 * blocks, tokens), jnp.float32),
            pltpu.VMEM((n_v, 2 * blocks, tokens), jnp.float32),
            dma,
            dma((n_h,)),
            dma(((n_v * n_h - 1) * cuts,)),
            dma((n_v * n_h * cuts,)),
            dma((n_v - 1,)),
            dma((n_v - 1,)),
            dma((n_h - 1,)),
            dma((n_h - 1,)),
            dma((n_v - 1,)),
            dma((n_v - 1,)),
        ],
        compiler_params=pltpu.CompilerParams(
            collective_id=0, has_side_effects=True, vmem_limit_bytes=60 * 2**20
        ),
    )(hidden.reshape(rows, depth), unembed, labels.reshape(1, tokens))


def solution(mesh):
    placed = (P(None, "vocab", "hid"), P(None, ("vocab", "hid")), P("vocab"))
    inner = functools.partial(body, n_v=mesh.shape["vocab"], n_h=mesh.shape["hid"])
    return jax.shard_map(inner, mesh=mesh, in_specs=placed, out_specs=(P(), P()), check_vma=False)
```

```python
import functools

import jax
import jax.numpy as jnp
from jax import lax
from jax.experimental import pallas as pl
from jax.experimental.pallas import tpu as pltpu
from jax.sharding import PartitionSpec as P

MESH = pl.DeviceIdType.MESH
LANES = 128
CUTS = 2
TILE = 2560
ORDER = (
    (0, 2, 0, 1), (0, 0, 1, 0), (0, 1, 0, 1), (0, 0, 1, 1), (0, 2, 0, 0), (0, 1, 0, 0),
    (2, 0, 0, 0), (1, 1, 0, 1), (1, 0, 1, 0), (1, 1, 0, 0), (1, 0, 1, 1), (1, 2, 0, 1),
    (1, 2, 0, 0), (2, 1, 0, 0), (1, 2, 1, 0), (3, 0, 0, 0), (1, 1, 1, 0), (1, 0, 2, 0),
    (2, 0, 1, 0), (1, 2, 1, 1), (1, 1, 1, 1), (1, 0, 2, 1), (3, 0, 0, 0), (2, 2, 0, 0),
    (3, 0, 0, 0), (2, 0, 2, 0), (2, 1, 1, 0), (1, 3, 0, 1), (1, 3, 1, 0), (1, 2, 2, 0),
    (1, 3, 0, 0), (1, 0, 3, 0), (1, 0, 3, 1), (2, 2, 1, 0), (1, 3, 1, 1), (2, 0, 3, 0),
    (1, 3, 2, 0), (1, 2, 2, 1), (2, 3, 0, 0), (2, 3, 1, 0), (1, 3, 2, 1), (1, 1, 3, 0),
    (1, 1, 2, 1), (1, 2, 3, 0), (1, 1, 2, 0), (2, 2, 2, 0), (1, 3, 3, 0), (1, 1, 3, 1),
    (1, 2, 3, 1), (2, 3, 2, 0), (2, 1, 2, 0), (1, 3, 3, 1), (2, 1, 3, 0), (2, 2, 3, 0),
    (3, 0, 0, 0), (2, 3, 3, 0),
)


def bits_of(mask):
    return [1 << b for b in range(mask.bit_length()) if mask >> b & 1]


def parent(group, slab):
    dims = bits_of(group)
    if group == 0:
        return (0, slab - 1), ("hid", 1)
    if len(dims) == 1:
        return (0, slab), ("vocab", group)
    if slab < len(dims):
        return (group ^ dims[slab], slab), ("vocab", dims[slab])
    return (group, slab - 1), ("hid", 1)


def depth_of(group, slab):
    return 0 if (group, slab) == (0, 0) else 1 + depth_of(*parent(group, slab)[0])


def plan(n_g, n_h, cuts):
    blocks = [(g, j) for j in range(n_h) for g in range(n_g) if (g, j) != (0, 0)]
    direct = [b for b in blocks if parent(*b)[0] == (0, 0)]
    ops = [("s", b, c) for c in range(cuts) for b in direct]
    arrived = {(0, 0)}
    done = set()

    def compute():
        for j in range(n_h):
            for g in range(n_g):
                need = {(g, j), (g, j - j % 2)}
                if (g, j) not in done and need <= arrived:
                    done.add((g, j))
                    ops.append(("c", g, j))

    compute()
    for b in sorted(blocks, key=lambda b: (depth_of(*b), b[1], b[0])):
        ops.extend(("w", b, c) for c in range(cuts))
        arrived.add(b)
        compute()
    return ops


def each(lo, hi, work):
    if hi - lo > 8:
        pl.loop(lo, hi)(work)
        return
    for i in range(lo, hi):
        work(i)


def flip(index, mask):
    for bit in bits_of(mask):
        index = index + bit - 2 * bit * lax.rem(index // bit, 2)
    return index


def combine(parts, blocks):
    sums = [part[0:blocks] for part in parts]
    top = functools.reduce(jnp.maximum, sums)
    total = sum(jnp.exp(own - top) for own in sums)
    return top + jnp.log(total), sum(part[blocks : 2 * blocks] for part in parts)


def kernel(
    n_v, n_h, layers,
    hid_hbm, w_hbm, lab_ref,
    loss_ref, mean_ref,
    buf, w, acc, labs, lanes, rel_stats, line, plane,
    own_sem, w_sem, send_sem, recv_sem, lab_send, lab_recv, line_send, line_recv, plane_send, plane_recv,
):
    v, z = lax.axis_index("vocab"), lax.axis_index("hid")
    rows = hid_hbm.shape[0]
    depth = hid_hbm.shape[1]
    cols = w_hbm.shape[1]
    first_col = (v * n_h + z) * cols
    dims = [1 << b for b in range((n_v // 2).bit_length() - 1)]
    groups = sorted(range(n_v // 2), key=lambda g: (len(bits_of(g)), g))
    pos = {2 * g + c: 2 * i + c for i, g in enumerate(groups) for c in range(2)}
    blocks = n_v * layers

    own = pltpu.make_async_copy(hid_hbm, buf.at[pl.ds(0, rows), pl.ds(0, depth)], own_sem)
    own.start()
    w_copies = []
    for s in range(n_h):
        src = lax.rem(z - s + n_h, n_h)
        copy = pltpu.make_async_copy(
            w_hbm.at[pl.ds(pl.multiple_of(src * depth, depth), depth)], w.at[pl.ds(s * depth, depth)], w_sem.at[s]
        )
        w_copies.append(copy)

    barrier = pltpu.get_barrier_semaphore()
    line_peers = [lax.rem(z + j, n_h) for j in range(1, n_h)]
    for peer in line_peers:
        pl.semaphore_signal(barrier, inc=1, device_id=(v, peer), device_id_type=MESH)
    for m in range(1, n_v):
        pl.semaphore_signal(barrier, inc=1, device_id=(flip(v, m), z), device_id_type=MESH)
    for copy in w_copies:
        copy.start()
    pl.semaphore_wait(barrier, n_h + n_v - 2)
    own.wait()

    cuts = CUTS if n_v * n_h <= 64 else 1
    piece = rows // cuts
    sends = []

    groups_at = {g: i for i, g in enumerate(groups)}
    children = {}
    for g in range(n_v // 2):
        for s in range(n_h):
            if (g, s) != (0, 0):
                source, hop = parent(g, s)
                children.setdefault(source, []).append(((g, s), hop))

    def block_copy(m, s, to_m, to_s, cut, device):
        k = min(len(sends), send_sem.shape[0] - 1)
        return pltpu.make_async_remote_copy(
            src_ref=buf.at[pl.ds(pos[m] * rows + cut * piece, piece), pl.ds(s * depth, depth)],
            dst_ref=buf.at[pl.ds(pos[to_m] * rows + cut * piece, piece), pl.ds(to_s * depth, depth)],
            send_sem=send_sem.at[k],
            recv_sem=recv_sem.at[(to_m * n_h + to_s) * cuts + cut],
            device_id=device, device_id_type=MESH,
        )

    def send(m, s, to_m, to_s, cut, device):
        copy = block_copy(m, s, to_m, to_s, cut, device)
        copy.start()
        sends.append(copy)

    def wait_block(m, s, cut):
        block_copy(m, s, m, s, cut, (flip(v, 1), z)).wait_recv()

    def hand_on(g, s, to, hop, cut):
        axis, mask = hop
        device = (v, lax.rem(z + mask, n_h)) if axis == "hid" else (flip(v, 2 * mask), z)
        send(2 * g, s, 2 * to[0], to[1], cut, device)

    def arrive(g, s, cut):
        wait_block(2 * g, s, cut)
        for to, hop in children.get((g, s), []):
            hand_on(g, s, to, hop, cut)
        send(2 * g, s, 2 * g + 1, s, cut, (flip(v, 1), z))

    tile = max(t for t in range(LANES, TILE + 1, LANES) if cols % t == 0)
    tiles = cols // tile
    waited = set()
    steps = {}

    def multiply(units):
        for g, s in units:
            for t in range(s - s % 2, s + 1):
                for cut in range(cuts):
                    if (g, t, cut) not in waited:
                        waited.add((g, t, cut))
                        wait_block(2 * g + 1, t, cut) if (g, t) != (0, 0) else wait_block(1, 0, cut)
                if t not in waited:
                    w_copies[t].wait()
                    waited.add(t)
        work = []
        for g, s in sorted(units, key=lambda unit: (unit[1], groups_at[unit[0]])):
            k_lo = s * depth // 256 * 256
            k_hi = (s + 1) * depth // 256 * 256 if s + 1 < n_h else n_h * depth
            first = g not in steps
            steps[g] = steps.get(g, 0) + 1
            work.append((groups_at[g], 1, k_lo, k_hi, first, steps[g] == n_h))
        jobs = []
        for at, count, k_lo, k_hi, first, last in work:
            for i, job in enumerate(jobs):
                if job[:2] == (at, count) and job[3] == k_lo and not job[5]:
                    jobs[i] = (at, count, job[2], k_hi, job[4], last)
                    break
            else:
                jobs.append((at, count, k_lo, k_hi, first, last))
        merged = []
        for job in jobs:
            if merged and merged[-1][0] + merged[-1][1] == job[0] and merged[-1][2:] == job[2:]:
                merged[-1] = (merged[-1][0], merged[-1][1] + job[1], *job[2:])
            else:
                merged.append(job)

        @pl.loop(0, tiles)
        def _(n):
            at = pl.ds(pl.multiple_of(n * tile, tile), tile)
            for row, count, k_lo, k_hi, first, last in merged:
                here = slice(row * 2 * rows, (row + count) * 2 * rows)
                value = jnp.dot(buf[here, k_lo:k_hi], w[k_lo:k_hi, at], preferred_element_type=jnp.float32)
                if not first:
                    value = acc[here, at] + value
                if not last:
                    acc[here, at] = value
                    continue
                chunks = [value[:, c : c + LANES] for c in range(0, tile, LANES)]
                old = lanes[0, here, :]
                peak = functools.reduce(jnp.maximum, chunks, old)
                total = lanes[1, here, :] * jnp.exp(old - peak)
                picked = lanes[2, here, :]
                wanted = lanes[3, here, :] - (n * tile).astype(jnp.float32)
                for i, x in enumerate(chunks):
                    total = total + jnp.exp(x - peak)
                    picked = picked + jnp.where(wanted == float(i * LANES), x, 0.0)
                lanes[0, here, :] = peak
                lanes[1, here, :] = total
                lanes[2, here, :] = picked

    def prepare():
        for copy in lab_copies:
            copy.wait()
        lane = (lax.broadcasted_iota(jnp.int32, (LANES, LANES), 1) + first_col).astype(jnp.float32)

        @functools.partial(each, 0, blocks)
        def _(p):
            at = pl.ds(p * LANES, LANES) if isinstance(p, int) else pl.ds(pl.multiple_of(p * LANES, LANES), LANES)
            label = jnp.broadcast_to(labs[p // layers].astype(jnp.float32), (LANES, LANES))
            lanes[0, at, :] = jnp.full((LANES, LANES), -jnp.inf, jnp.float32)
            lanes[1, at, :] = jnp.zeros((LANES, LANES), jnp.float32)
            lanes[2, at, :] = jnp.zeros((LANES, LANES), jnp.float32)
            lanes[3, at, :] = jnp.transpose(label) - lane

    def stats(first, count):
        @functools.partial(each, first * 2 * layers, (first + count) * 2 * layers)
        def _(p):
            at = pl.ds(p * LANES, LANES) if isinstance(p, int) else pl.ds(pl.multiple_of(p * LANES, LANES), LANES)
            peak = jnp.transpose(lanes[0, at, :])
            row_peak = jnp.max(peak, axis=0, keepdims=True)
            total = jnp.transpose(lanes[1, at, :]) * jnp.exp(peak - row_peak)
            rel_stats[0, p] = row_peak + jnp.log(jnp.sum(total, axis=0, keepdims=True))
            rel_stats[1, p] = jnp.sum(jnp.transpose(lanes[2, at, :]), axis=0, keepdims=True)

    lab_copies = []
    for m in range(1, n_v):
        copy = pltpu.make_async_remote_copy(
            src_ref=lab_ref, dst_ref=labs.at[pos[m]],
            send_sem=lab_send.at[m - 1], recv_sem=lab_recv.at[m - 1],
            device_id=(flip(v, m), z), device_id_type=MESH,
        )
        copy.start()
        lab_copies.append(copy)
    labs[0] = lab_ref[...]

    ops = plan(n_v // 2, n_h, cuts)
    tuned = [("cb"[kind - 2], g, s) if kind > 1 else ("sw"[kind], (g, s), cut) for kind, g, s, cut in ORDER]
    if sorted(map(str, ops)) == sorted(str(op) for op in tuned if op[0] != "b"):
        ops = tuned
    begin = 0
    while ops[begin][0] == "s":
        begin += 1
    for _, (g, s), cut in ops[:begin]:
        hand_on(0, 0, (g, s), parent(g, s)[1], cut)
    for cut in range(cuts):
        send(0, 0, 1, 0, cut, (flip(v, 1), z))
    units, prepared, known = [], [], set()
    for op in ops[begin:] + [None]:
        if op is not None and op[0] == "c":
            units.append(op[1:])
            continue
        if units:
            if not prepared and any(steps.get(g, 0) + sum(u[0] == g for u in units) == n_h for g, _ in units):
                prepare()
                prepared.append(True)
            multiply(units)
            for g, _ in units:
                if op is not None and steps[g] == n_h and g not in known:
                    known.add(g)
                    stats(groups_at[g], 1)
            units = []
        if op is None:
            break
        if op[0] == "b":
            continue
        if op[0] == "s":
            hand_on(0, 0, op[1], parent(*op[1])[1], op[2])
        else:
            arrive(*op[1], op[2])
    rest = [i for i, g in enumerate(groups) if g not in known]
    while rest:
        count = 1
        while count < len(rest) and rest[count] == rest[0] + count:
            count += 1
        stats(rest[0], count)
        rest = rest[count:]

    for m in range(n_v):
        for l in range(layers):
            for k in range(2):
                line[z, pl.ds(k * blocks + flip(v, m) * layers + l, 1), :] = rel_stats[k, pos[m] * layers + l]
    line_copies = []
    for j, peer in enumerate(line_peers):
        copy = pltpu.make_async_remote_copy(
            src_ref=line.at[z], dst_ref=line.at[z],
            send_sem=line_send.at[j], recv_sem=line_recv.at[j],
            device_id=(v, peer), device_id_type=MESH,
        )
        copy.start()
        line_copies.append(copy)
    for copy in line_copies:
        copy.wait_recv()
    whole, picked = combine([line[h] for h in range(n_h)], blocks)
    plane[v, 0:blocks, :] = whole
    plane[v, blocks : 2 * blocks, :] = picked
    plane_copies = []
    for m in range(1, n_v):
        copy = pltpu.make_async_remote_copy(
            src_ref=plane.at[v], dst_ref=plane.at[v],
            send_sem=plane_send.at[m - 1], recv_sem=plane_recv.at[m - 1],
            device_id=(flip(v, m), z), device_id_type=MESH,
        )
        copy.start()
        plane_copies.append(copy)
    for copy in sends + line_copies:
        copy.wait_send()
    for copy in plane_copies:
        copy.wait_recv()
    whole, picked = combine([plane[u] for u in range(n_v)], blocks)
    loss = whole - picked
    for l in range(layers):
        sums = jnp.zeros((1, LANES), jnp.float32)
        for u in range(n_v):
            row = loss[u * layers + l : u * layers + l + 1]
            loss_ref[l : l + 1, u * LANES : (u + 1) * LANES] = row
            sums = sums + row
        mean_ref[l] = jnp.sum(sums) / (n_v * LANES)
    for copy in plane_copies:
        copy.wait_send()


def body(hidden, unembed, labels, n_v, n_h):
    layers, tokens, depth = hidden.shape
    cols = unembed.shape[1]
    rows = layers * tokens
    blocks = n_v * layers
    dma = pltpu.SemaphoreType.DMA
    any_space = pl.BlockSpec(memory_space=pl.ANY)
    vmem = pl.BlockSpec(memory_space=pltpu.VMEM)
    cuts = CUTS if n_v * n_h <= 64 else 1
    return pl.pallas_call(
        functools.partial(kernel, n_v, n_h, layers),
        out_shape=(
            jax.ShapeDtypeStruct((layers, n_v * tokens), jnp.float32),
            jax.ShapeDtypeStruct((layers,), jnp.float32),
        ),
        in_specs=[any_space, any_space, vmem],
        out_specs=(vmem, pl.BlockSpec(memory_space=pltpu.SMEM)),
        scratch_shapes=[
            pltpu.VMEM((n_v * rows, n_h * depth), jnp.bfloat16),
            pltpu.VMEM((n_h * depth, cols), jnp.bfloat16),
            pltpu.VMEM((n_v * rows, cols), jnp.float32),
            pltpu.VMEM((n_v, 1, tokens), jnp.int32),
            pltpu.VMEM((4, n_v * rows, LANES), jnp.float32),
            pltpu.VMEM((2, blocks, 1, tokens), jnp.float32),
            pltpu.VMEM((n_h, 2 * blocks, tokens), jnp.float32),
            pltpu.VMEM((n_v, 2 * blocks, tokens), jnp.float32),
            dma,
            dma((n_h,)),
            dma(((n_v * n_h - 1) * cuts,)),
            dma((n_v * n_h * cuts,)),
            dma((n_v - 1,)),
            dma((n_v - 1,)),
            dma((n_h - 1,)),
            dma((n_h - 1,)),
            dma((n_v - 1,)),
            dma((n_v - 1,)),
        ],
        compiler_params=pltpu.CompilerParams(
            collective_id=0, has_side_effects=True, vmem_limit_bytes=60 * 2**20
        ),
    )(hidden.reshape(rows, depth), unembed, labels.reshape(1, tokens))


def solution(mesh):
    placed = (P(None, "vocab", "hid"), P(None, ("vocab", "hid")), P("vocab"))
    inner = functools.partial(body, n_v=mesh.shape["vocab"], n_h=mesh.shape["hid"])
    return jax.shard_map(inner, mesh=mesh, in_specs=placed, out_specs=(P(), P()), check_vma=False)
```

```python
import functools

import jax
import jax.numpy as jnp
from jax import lax
from jax.experimental import pallas as pl
from jax.experimental.pallas import tpu as pltpu
from jax.sharding import PartitionSpec as P

MESH = pl.DeviceIdType.MESH
LANES = 128
CUTS = 2
TILE = 2560
ORDER = (
    (0, 0, 1, 1), (0, 1, 0, 0), (0, 2, 0, 0), (0, 2, 0, 1), (2, 0, 0, 0), (0, 0, 1, 0),
    (0, 1, 0, 1), (1, 0, 1, 1), (1, 1, 0, 0), (1, 1, 0, 1), (1, 0, 1, 0), (1, 2, 0, 1),
    (1, 2, 0, 0), (2, 1, 0, 0), (1, 1, 1, 1), (1, 2, 1, 1), (1, 0, 2, 1), (2, 0, 1, 0),
    (1, 2, 1, 0), (1, 1, 1, 0), (1, 0, 2, 0), (2, 2, 0, 0), (3, 0, 0, 0), (3, 0, 0, 0),
    (2, 1, 1, 0), (1, 3, 0, 1), (1, 3, 1, 1), (2, 2, 1, 0), (1, 3, 0, 0), (1, 0, 3, 0),
    (1, 0, 3, 1), (1, 2, 2, 1), (2, 0, 2, 0), (1, 1, 2, 1), (1, 3, 1, 0), (2, 3, 0, 0),
    (2, 0, 3, 0), (1, 2, 2, 0), (1, 3, 2, 1), (1, 1, 2, 0), (2, 3, 1, 0), (1, 2, 3, 0),
    (1, 3, 2, 0), (1, 1, 3, 0), (2, 2, 2, 0), (2, 1, 2, 0), (1, 2, 3, 1), (2, 3, 2, 0),
    (1, 3, 3, 1), (1, 1, 3, 1), (2, 2, 3, 0), (1, 3, 3, 0), (2, 1, 3, 0), (3, 0, 0, 0),
    (3, 0, 0, 0), (2, 3, 3, 0),
)


def bits_of(mask):
    return [1 << b for b in range(mask.bit_length()) if mask >> b & 1]


def parent(group, slab):
    dims = bits_of(group)
    if group == 0:
        return (0, slab - 1), ("hid", 1)
    if len(dims) == 1:
        return (0, slab), ("vocab", group)
    if slab < len(dims):
        return (group ^ dims[slab], slab), ("vocab", dims[slab])
    return (group, slab - 1), ("hid", 1)


def depth_of(group, slab):
    return 0 if (group, slab) == (0, 0) else 1 + depth_of(*parent(group, slab)[0])


def plan(n_g, n_h, cuts):
    blocks = [(g, j) for j in range(n_h) for g in range(n_g) if (g, j) != (0, 0)]
    direct = [b for b in blocks if parent(*b)[0] == (0, 0)]
    ops = [("s", b, c) for c in range(cuts) for b in direct]
    arrived = {(0, 0)}
    done = set()

    def compute():
        for j in range(n_h):
            for g in range(n_g):
                need = {(g, j), (g, j - j % 2)}
                if (g, j) not in done and need <= arrived:
                    done.add((g, j))
                    ops.append(("c", g, j))

    compute()
    for b in sorted(blocks, key=lambda b: (depth_of(*b), b[1], b[0])):
        ops.extend(("w", b, c) for c in range(cuts))
        arrived.add(b)
        compute()
    return ops


def each(lo, hi, work):
    if hi - lo > 8:
        pl.loop(lo, hi)(work)
        return
    for i in range(lo, hi):
        work(i)


def flip(index, mask):
    for bit in bits_of(mask):
        index = index + bit - 2 * bit * lax.rem(index // bit, 2)
    return index


def combine(parts, blocks):
    sums = [part[0:blocks] for part in parts]
    top = functools.reduce(jnp.maximum, sums)
    total = sum(jnp.exp(own - top) for own in sums)
    return top + jnp.log(total), sum(part[blocks : 2 * blocks] for part in parts)


def kernel(
    n_v, n_h, layers,
    hid_hbm, w_hbm, lab_ref,
    loss_ref, mean_ref,
    buf, w, acc, labs, lanes, rel_stats, line, plane,
    own_sem, w_sem, send_sem, recv_sem, lab_send, lab_recv, line_send, line_recv, plane_send, plane_recv,
):
    v, z = lax.axis_index("vocab"), lax.axis_index("hid")
    rows = hid_hbm.shape[0]
    depth = hid_hbm.shape[1]
    cols = w_hbm.shape[1]
    first_col = (v * n_h + z) * cols
    dims = [1 << b for b in range((n_v // 2).bit_length() - 1)]
    groups = sorted(range(n_v // 2), key=lambda g: (len(bits_of(g)), g))
    pos = {2 * g + c: 2 * i + c for i, g in enumerate(groups) for c in range(2)}
    blocks = n_v * layers

    own = pltpu.make_async_copy(hid_hbm, buf.at[pl.ds(0, rows), pl.ds(0, depth)], own_sem)
    own.start()
    w_copies = []
    for s in range(n_h):
        src = lax.rem(z - s + n_h, n_h)
        copy = pltpu.make_async_copy(
            w_hbm.at[pl.ds(pl.multiple_of(src * depth, depth), depth)], w.at[pl.ds(s * depth, depth)], w_sem.at[s]
        )
        w_copies.append(copy)

    barrier = pltpu.get_barrier_semaphore()
    line_peers = [lax.rem(z + j, n_h) for j in range(1, n_h)]
    for peer in line_peers:
        pl.semaphore_signal(barrier, inc=1, device_id=(v, peer), device_id_type=MESH)
    for m in range(1, n_v):
        pl.semaphore_signal(barrier, inc=1, device_id=(flip(v, m), z), device_id_type=MESH)
    for copy in w_copies:
        copy.start()
    pl.semaphore_wait(barrier, n_h + n_v - 2)
    own.wait()

    cuts = CUTS if n_v * n_h <= 64 else 1
    piece = rows // cuts
    sends = []

    groups_at = {g: i for i, g in enumerate(groups)}
    children = {}
    for g in range(n_v // 2):
        for s in range(n_h):
            if (g, s) != (0, 0):
                source, hop = parent(g, s)
                children.setdefault(source, []).append(((g, s), hop))

    def block_copy(m, s, to_m, to_s, cut, device):
        k = min(len(sends), send_sem.shape[0] - 1)
        return pltpu.make_async_remote_copy(
            src_ref=buf.at[pl.ds(pos[m] * rows + cut * piece, piece), pl.ds(s * depth, depth)],
            dst_ref=buf.at[pl.ds(pos[to_m] * rows + cut * piece, piece), pl.ds(to_s * depth, depth)],
            send_sem=send_sem.at[k],
            recv_sem=recv_sem.at[(to_m * n_h + to_s) * cuts + cut],
            device_id=device, device_id_type=MESH,
        )

    def send(m, s, to_m, to_s, cut, device):
        copy = block_copy(m, s, to_m, to_s, cut, device)
        copy.start()
        sends.append(copy)

    def wait_block(m, s, cut):
        block_copy(m, s, m, s, cut, (flip(v, 1), z)).wait_recv()

    def hand_on(g, s, to, hop, cut):
        axis, mask = hop
        device = (v, lax.rem(z + mask, n_h)) if axis == "hid" else (flip(v, 2 * mask), z)
        send(2 * g, s, 2 * to[0], to[1], cut, device)

    def arrive(g, s, cut):
        wait_block(2 * g, s, cut)
        for to, hop in children.get((g, s), []):
            hand_on(g, s, to, hop, cut)
        send(2 * g, s, 2 * g + 1, s, cut, (flip(v, 1), z))

    tile = max(t for t in range(LANES, TILE + 1, LANES) if cols % t == 0)
    tiles = cols // tile
    waited = set()
    steps = {}

    def multiply(units):
        for g, s in units:
            for t in range(s - s % 2, s + 1):
                for cut in range(cuts):
                    if (g, t, cut) not in waited:
                        waited.add((g, t, cut))
                        wait_block(2 * g + 1, t, cut) if (g, t) != (0, 0) else wait_block(1, 0, cut)
                if t not in waited:
                    w_copies[t].wait()
                    waited.add(t)
        work = []
        for g, s in sorted(units, key=lambda unit: (unit[1], groups_at[unit[0]])):
            k_lo = s * depth // 256 * 256
            k_hi = (s + 1) * depth // 256 * 256 if s + 1 < n_h else n_h * depth
            first = g not in steps
            steps[g] = steps.get(g, 0) + 1
            work.append((groups_at[g], 1, k_lo, k_hi, first, steps[g] == n_h))
        jobs = []
        for at, count, k_lo, k_hi, first, last in work:
            for i, job in enumerate(jobs):
                if job[:2] == (at, count) and job[3] == k_lo and not job[5]:
                    jobs[i] = (at, count, job[2], k_hi, job[4], last)
                    break
            else:
                jobs.append((at, count, k_lo, k_hi, first, last))
        merged = []
        for job in jobs:
            if merged and merged[-1][0] + merged[-1][1] == job[0] and merged[-1][2:] == job[2:]:
                merged[-1] = (merged[-1][0], merged[-1][1] + job[1], *job[2:])
            else:
                merged.append(job)

        @functools.partial(each, 0, tiles)
        def _(n):
            at = pl.ds(n * tile, tile) if isinstance(n, int) else pl.ds(pl.multiple_of(n * tile, tile), tile)
            for row, count, k_lo, k_hi, first, last in merged:
                here = slice(row * 2 * rows, (row + count) * 2 * rows)
                value = jnp.dot(buf[here, k_lo:k_hi], w[k_lo:k_hi, at], preferred_element_type=jnp.float32)
                if not first:
                    value = acc[here, at] + value
                if not last:
                    acc[here, at] = value
                    continue
                chunks = [value[:, c : c + LANES] for c in range(0, tile, LANES)]
                old = lanes[0, here, :]
                peak = functools.reduce(jnp.maximum, chunks, old)
                total = lanes[1, here, :] * jnp.exp(old - peak)
                picked = lanes[2, here, :]
                wanted = lanes[3, here, :] - jnp.float32(n * tile)
                for i, x in enumerate(chunks):
                    total = total + jnp.exp(x - peak)
                    picked = picked + jnp.where(wanted == float(i * LANES), x, 0.0)
                lanes[0, here, :] = peak
                lanes[1, here, :] = total
                lanes[2, here, :] = picked

    def prepare():
        for copy in lab_copies:
            copy.wait()
        lane = (lax.broadcasted_iota(jnp.int32, (LANES, LANES), 1) + first_col).astype(jnp.float32)

        @functools.partial(each, 0, blocks)
        def _(p):
            at = pl.ds(p * LANES, LANES) if isinstance(p, int) else pl.ds(pl.multiple_of(p * LANES, LANES), LANES)
            label = jnp.broadcast_to(labs[p // layers].astype(jnp.float32), (LANES, LANES))
            lanes[0, at, :] = jnp.full((LANES, LANES), -jnp.inf, jnp.float32)
            lanes[1, at, :] = jnp.zeros((LANES, LANES), jnp.float32)
            lanes[2, at, :] = jnp.zeros((LANES, LANES), jnp.float32)
            lanes[3, at, :] = jnp.transpose(label) - lane

    def stats(first, count):
        @functools.partial(each, first * 2 * layers, (first + count) * 2 * layers)
        def _(p):
            at = pl.ds(p * LANES, LANES) if isinstance(p, int) else pl.ds(pl.multiple_of(p * LANES, LANES), LANES)
            peak = jnp.transpose(lanes[0, at, :])
            row_peak = jnp.max(peak, axis=0, keepdims=True)
            total = jnp.transpose(lanes[1, at, :]) * jnp.exp(peak - row_peak)
            rel_stats[0, p] = row_peak + jnp.log(jnp.sum(total, axis=0, keepdims=True))
            rel_stats[1, p] = jnp.sum(jnp.transpose(lanes[2, at, :]), axis=0, keepdims=True)

    lab_copies = []
    for m in range(1, n_v):
        copy = pltpu.make_async_remote_copy(
            src_ref=lab_ref, dst_ref=labs.at[pos[m]],
            send_sem=lab_send.at[m - 1], recv_sem=lab_recv.at[m - 1],
            device_id=(flip(v, m), z), device_id_type=MESH,
        )
        copy.start()
        lab_copies.append(copy)
    labs[0] = lab_ref[...]

    ops = plan(n_v // 2, n_h, cuts)
    tuned = [("cb"[kind - 2], g, s) if kind > 1 else ("sw"[kind], (g, s), cut) for kind, g, s, cut in ORDER]
    if sorted(map(str, ops)) == sorted(str(op) for op in tuned if op[0] != "b"):
        ops = tuned
    begin = 0
    while ops[begin][0] == "s":
        begin += 1
    for _, (g, s), cut in ops[:begin]:
        hand_on(0, 0, (g, s), parent(g, s)[1], cut)
    for cut in range(cuts):
        send(0, 0, 1, 0, cut, (flip(v, 1), z))
    units, prepared, known = [], [], set()
    for op in ops[begin:] + [None]:
        if op is not None and op[0] == "c":
            units.append(op[1:])
            continue
        if units:
            if not prepared and any(steps.get(g, 0) + sum(u[0] == g for u in units) == n_h for g, _ in units):
                prepare()
                prepared.append(True)
            multiply(units)
            for g, _ in units:
                if op is not None and steps[g] == n_h and g not in known:
                    known.add(g)
                    stats(groups_at[g], 1)
            units = []
        if op is None:
            break
        if op[0] == "b":
            continue
        if op[0] == "s":
            hand_on(0, 0, op[1], parent(*op[1])[1], op[2])
        else:
            arrive(*op[1], op[2])
    rest = [i for i, g in enumerate(groups) if g not in known]
    while rest:
        count = 1
        while count < len(rest) and rest[count] == rest[0] + count:
            count += 1
        stats(rest[0], count)
        rest = rest[count:]

    for m in range(n_v):
        for l in range(layers):
            for k in range(2):
                line[z, pl.ds(k * blocks + flip(v, m) * layers + l, 1), :] = rel_stats[k, pos[m] * layers + l]
    line_copies = []
    for j, peer in enumerate(line_peers):
        copy = pltpu.make_async_remote_copy(
            src_ref=line.at[z], dst_ref=line.at[z],
            send_sem=line_send.at[j], recv_sem=line_recv.at[j],
            device_id=(v, peer), device_id_type=MESH,
        )
        copy.start()
        line_copies.append(copy)
    for copy in line_copies:
        copy.wait_recv()
    whole, picked = combine([line[h] for h in range(n_h)], blocks)
    plane[v, 0:blocks, :] = whole
    plane[v, blocks : 2 * blocks, :] = picked
    plane_copies = []
    for m in range(1, n_v):
        copy = pltpu.make_async_remote_copy(
            src_ref=plane.at[v], dst_ref=plane.at[v],
            send_sem=plane_send.at[m - 1], recv_sem=plane_recv.at[m - 1],
            device_id=(flip(v, m), z), device_id_type=MESH,
        )
        copy.start()
        plane_copies.append(copy)
    for copy in sends + line_copies:
        copy.wait_send()
    for copy in plane_copies:
        copy.wait_recv()
    whole, picked = combine([plane[u] for u in range(n_v)], blocks)
    loss = whole - picked
    for l in range(layers):
        sums = jnp.zeros((1, LANES), jnp.float32)
        for u in range(n_v):
            row = loss[u * layers + l : u * layers + l + 1]
            loss_ref[l : l + 1, u * LANES : (u + 1) * LANES] = row
            sums = sums + row
        mean_ref[l] = jnp.sum(sums) / (n_v * LANES)
    for copy in plane_copies:
        copy.wait_send()


def body(hidden, unembed, labels, n_v, n_h):
    layers, tokens, depth = hidden.shape
    cols = unembed.shape[1]
    rows = layers * tokens
    blocks = n_v * layers
    dma = pltpu.SemaphoreType.DMA
    any_space = pl.BlockSpec(memory_space=pl.ANY)
    vmem = pl.BlockSpec(memory_space=pltpu.VMEM)
    cuts = CUTS if n_v * n_h <= 64 else 1
    return pl.pallas_call(
        functools.partial(kernel, n_v, n_h, layers),
        out_shape=(
            jax.ShapeDtypeStruct((layers, n_v * tokens), jnp.float32),
            jax.ShapeDtypeStruct((layers,), jnp.float32),
        ),
        in_specs=[any_space, any_space, vmem],
        out_specs=(vmem, pl.BlockSpec(memory_space=pltpu.SMEM)),
        scratch_shapes=[
            pltpu.VMEM((n_v * rows, n_h * depth), jnp.bfloat16),
            pltpu.VMEM((n_h * depth, cols), jnp.bfloat16),
            pltpu.VMEM((n_v * rows, cols), jnp.float32),
            pltpu.VMEM((n_v, 1, tokens), jnp.int32),
            pltpu.VMEM((4, n_v * rows, LANES), jnp.float32),
            pltpu.VMEM((2, blocks, 1, tokens), jnp.float32),
            pltpu.VMEM((n_h, 2 * blocks, tokens), jnp.float32),
            pltpu.VMEM((n_v, 2 * blocks, tokens), jnp.float32),
            dma,
            dma((n_h,)),
            dma(((n_v * n_h - 1) * cuts,)),
            dma((n_v * n_h * cuts,)),
            dma((n_v - 1,)),
            dma((n_v - 1,)),
            dma((n_h - 1,)),
            dma((n_h - 1,)),
            dma((n_v - 1,)),
            dma((n_v - 1,)),
        ],
        compiler_params=pltpu.CompilerParams(
            collective_id=0, has_side_effects=True, vmem_limit_bytes=60 * 2**20
        ),
    )(hidden.reshape(rows, depth), unembed, labels.reshape(1, tokens))


def solution(mesh):
    placed = (P(None, "vocab", "hid"), P(None, ("vocab", "hid")), P("vocab"))
    inner = functools.partial(body, n_v=mesh.shape["vocab"], n_h=mesh.shape["hid"])
    return jax.shard_map(inner, mesh=mesh, in_specs=placed, out_specs=(P(), P()), check_vma=False)
```

```python
import functools

import jax
import jax.numpy as jnp
from jax import lax
from jax.experimental import pallas as pl
from jax.experimental.pallas import tpu as pltpu
from jax.sharding import PartitionSpec as P

MESH = pl.DeviceIdType.MESH
LANES = 128
CUTS = 2
TILE = 1280
ORDER = (
    (0, 0, 1, 1), (0, 1, 0, 0), (0, 2, 0, 0), (0, 2, 0, 1), (2, 0, 0, 0), (0, 0, 1, 0),
    (0, 1, 0, 1), (1, 0, 1, 1), (1, 1, 0, 0), (1, 1, 0, 1), (1, 0, 1, 0), (1, 2, 0, 1),
    (1, 2, 0, 0), (2, 1, 0, 0), (1, 1, 1, 1), (1, 2, 1, 1), (1, 0, 2, 1), (2, 0, 1, 0),
    (1, 2, 1, 0), (1, 1, 1, 0), (1, 0, 2, 0), (2, 2, 0, 0), (3, 0, 0, 0), (3, 0, 0, 0),
    (2, 1, 1, 0), (1, 3, 0, 1), (1, 3, 1, 1), (2, 2, 1, 0), (1, 3, 0, 0), (1, 0, 3, 0),
    (1, 0, 3, 1), (1, 2, 2, 1), (2, 0, 2, 0), (1, 1, 2, 1), (1, 3, 1, 0), (2, 3, 0, 0),
    (2, 0, 3, 0), (1, 2, 2, 0), (1, 3, 2, 1), (1, 1, 2, 0), (2, 3, 1, 0), (1, 2, 3, 0),
    (1, 3, 2, 0), (1, 1, 3, 0), (2, 2, 2, 0), (2, 1, 2, 0), (1, 2, 3, 1), (2, 3, 2, 0),
    (1, 3, 3, 1), (1, 1, 3, 1), (2, 2, 3, 0), (1, 3, 3, 0), (2, 1, 3, 0), (3, 0, 0, 0),
    (3, 0, 0, 0), (2, 3, 3, 0),
)


def bits_of(mask):
    return [1 << b for b in range(mask.bit_length()) if mask >> b & 1]


def parent(group, slab):
    dims = bits_of(group)
    if group == 0:
        return (0, slab - 1), ("hid", 1)
    if len(dims) == 1:
        return (0, slab), ("vocab", group)
    if slab < len(dims):
        return (group ^ dims[slab], slab), ("vocab", dims[slab])
    return (group, slab - 1), ("hid", 1)


def depth_of(group, slab):
    return 0 if (group, slab) == (0, 0) else 1 + depth_of(*parent(group, slab)[0])


def plan(n_g, n_h, cuts):
    blocks = [(g, j) for j in range(n_h) for g in range(n_g) if (g, j) != (0, 0)]
    direct = [b for b in blocks if parent(*b)[0] == (0, 0)]
    ops = [("s", b, c) for c in range(cuts) for b in direct]
    arrived = {(0, 0)}
    done = set()

    def compute():
        for j in range(n_h):
            for g in range(n_g):
                need = {(g, j), (g, j - j % 2)}
                if (g, j) not in done and need <= arrived:
                    done.add((g, j))
                    ops.append(("c", g, j))

    compute()
    for b in sorted(blocks, key=lambda b: (depth_of(*b), b[1], b[0])):
        ops.extend(("w", b, c) for c in range(cuts))
        arrived.add(b)
        compute()
    return ops


def each(lo, hi, work):
    if hi - lo > 8:
        pl.loop(lo, hi)(work)
        return
    for i in range(lo, hi):
        work(i)


def flip(index, mask):
    for bit in bits_of(mask):
        index = index + bit - 2 * bit * lax.rem(index // bit, 2)
    return index


def combine(parts, blocks):
    sums = [part[0:blocks] for part in parts]
    top = functools.reduce(jnp.maximum, sums)
    total = sum(jnp.exp(own - top) for own in sums)
    return top + jnp.log(total), sum(part[blocks : 2 * blocks] for part in parts)


def kernel(
    n_v, n_h, layers,
    hid_hbm, w_hbm, lab_ref,
    loss_ref, mean_ref,
    buf, w, acc, labs, lanes, rel_stats, line, plane,
    own_sem, w_sem, send_sem, recv_sem, lab_send, lab_recv, line_send, line_recv, plane_send, plane_recv,
):
    v, z = lax.axis_index("vocab"), lax.axis_index("hid")
    rows = hid_hbm.shape[0]
    depth = hid_hbm.shape[1]
    cols = w_hbm.shape[1]
    first_col = (v * n_h + z) * cols
    dims = [1 << b for b in range((n_v // 2).bit_length() - 1)]
    groups = sorted(range(n_v // 2), key=lambda g: (len(bits_of(g)), g))
    pos = {2 * g + c: 2 * i + c for i, g in enumerate(groups) for c in range(2)}
    blocks = n_v * layers

    own = pltpu.make_async_copy(hid_hbm, buf.at[pl.ds(0, rows), pl.ds(0, depth)], own_sem)
    own.start()
    w_copies = []
    for s in range(n_h):
        src = lax.rem(z - s + n_h, n_h)
        copy = pltpu.make_async_copy(
            w_hbm.at[pl.ds(pl.multiple_of(src * depth, depth), depth)], w.at[pl.ds(s * depth, depth)], w_sem.at[s]
        )
        w_copies.append(copy)

    barrier = pltpu.get_barrier_semaphore()
    line_peers = [lax.rem(z + j, n_h) for j in range(1, n_h)]
    for peer in line_peers:
        pl.semaphore_signal(barrier, inc=1, device_id=(v, peer), device_id_type=MESH)
    for m in range(1, n_v):
        pl.semaphore_signal(barrier, inc=1, device_id=(flip(v, m), z), device_id_type=MESH)
    for copy in w_copies:
        copy.start()
    pl.semaphore_wait(barrier, n_h + n_v - 2)
    own.wait()

    cuts = CUTS if n_v * n_h <= 64 else 1
    piece = rows // cuts
    sends = []

    groups_at = {g: i for i, g in enumerate(groups)}
    children = {}
    for g in range(n_v // 2):
        for s in range(n_h):
            if (g, s) != (0, 0):
                source, hop = parent(g, s)
                children.setdefault(source, []).append(((g, s), hop))

    def block_copy(m, s, to_m, to_s, cut, device):
        k = min(len(sends), send_sem.shape[0] - 1)
        return pltpu.make_async_remote_copy(
            src_ref=buf.at[pl.ds(pos[m] * rows + cut * piece, piece), pl.ds(s * depth, depth)],
            dst_ref=buf.at[pl.ds(pos[to_m] * rows + cut * piece, piece), pl.ds(to_s * depth, depth)],
            send_sem=send_sem.at[k],
            recv_sem=recv_sem.at[(to_m * n_h + to_s) * cuts + cut],
            device_id=device, device_id_type=MESH,
        )

    def send(m, s, to_m, to_s, cut, device):
        copy = block_copy(m, s, to_m, to_s, cut, device)
        copy.start()
        sends.append(copy)

    def wait_block(m, s, cut):
        block_copy(m, s, m, s, cut, (flip(v, 1), z)).wait_recv()

    def hand_on(g, s, to, hop, cut):
        axis, mask = hop
        device = (v, lax.rem(z + mask, n_h)) if axis == "hid" else (flip(v, 2 * mask), z)
        send(2 * g, s, 2 * to[0], to[1], cut, device)

    def arrive(g, s, cut):
        wait_block(2 * g, s, cut)
        for to, hop in children.get((g, s), []):
            hand_on(g, s, to, hop, cut)
        send(2 * g, s, 2 * g + 1, s, cut, (flip(v, 1), z))

    tile = max(t for t in range(LANES, TILE + 1, LANES) if cols % t == 0)
    tiles = cols // tile
    waited = set()
    steps = {}

    def multiply(units):
        for g, s in units:
            for t in range(s - s % 2, s + 1):
                for cut in range(cuts):
                    if (g, t, cut) not in waited:
                        waited.add((g, t, cut))
                        wait_block(2 * g + 1, t, cut) if (g, t) != (0, 0) else wait_block(1, 0, cut)
                if t not in waited:
                    w_copies[t].wait()
                    waited.add(t)
        work = []
        for g, s in sorted(units, key=lambda unit: (unit[1], groups_at[unit[0]])):
            k_lo = s * depth // 256 * 256
            k_hi = (s + 1) * depth // 256 * 256 if s + 1 < n_h else n_h * depth
            first = g not in steps
            steps[g] = steps.get(g, 0) + 1
            work.append((groups_at[g], 1, k_lo, k_hi, first, steps[g] == n_h))
        jobs = []
        for at, count, k_lo, k_hi, first, last in work:
            for i, job in enumerate(jobs):
                if job[:2] == (at, count) and job[3] == k_lo and not job[5]:
                    jobs[i] = (at, count, job[2], k_hi, job[4], last)
                    break
            else:
                jobs.append((at, count, k_lo, k_hi, first, last))
        merged = []
        for job in jobs:
            if merged and merged[-1][0] + merged[-1][1] == job[0] and merged[-1][2:] == job[2:]:
                merged[-1] = (merged[-1][0], merged[-1][1] + job[1], *job[2:])
            else:
                merged.append(job)

        @functools.partial(each, 0, tiles)
        def _(n):
            at = pl.ds(n * tile, tile) if isinstance(n, int) else pl.ds(pl.multiple_of(n * tile, tile), tile)
            for row, count, k_lo, k_hi, first, last in merged:
                here = slice(row * 2 * rows, (row + count) * 2 * rows)
                value = jnp.dot(buf[here, k_lo:k_hi], w[k_lo:k_hi, at], preferred_element_type=jnp.float32)
                if not first:
                    value = acc[here, at] + value
                if not last:
                    acc[here, at] = value
                    continue
                chunks = [value[:, c : c + LANES] for c in range(0, tile, LANES)]
                old = lanes[0, here, :]
                peak = functools.reduce(jnp.maximum, chunks, old)
                total = lanes[1, here, :] * jnp.exp(old - peak)
                picked = lanes[2, here, :]
                wanted = lanes[3, here, :] - jnp.float32(n * tile)
                for i, x in enumerate(chunks):
                    total = total + jnp.exp(x - peak)
                    picked = picked + jnp.where(wanted == float(i * LANES), x, 0.0)
                lanes[0, here, :] = peak
                lanes[1, here, :] = total
                lanes[2, here, :] = picked

    def prepare():
        for copy in lab_copies:
            copy.wait()
        lane = (lax.broadcasted_iota(jnp.int32, (LANES, LANES), 1) + first_col).astype(jnp.float32)

        @functools.partial(each, 0, blocks)
        def _(p):
            at = pl.ds(p * LANES, LANES) if isinstance(p, int) else pl.ds(pl.multiple_of(p * LANES, LANES), LANES)
            label = jnp.broadcast_to(labs[p // layers].astype(jnp.float32), (LANES, LANES))
            lanes[0, at, :] = jnp.full((LANES, LANES), -jnp.inf, jnp.float32)
            lanes[1, at, :] = jnp.zeros((LANES, LANES), jnp.float32)
            lanes[2, at, :] = jnp.zeros((LANES, LANES), jnp.float32)
            lanes[3, at, :] = jnp.transpose(label) - lane

    def stats(first, count):
        @functools.partial(each, first * 2 * layers, (first + count) * 2 * layers)
        def _(p):
            at = pl.ds(p * LANES, LANES) if isinstance(p, int) else pl.ds(pl.multiple_of(p * LANES, LANES), LANES)
            peak = jnp.transpose(lanes[0, at, :])
            row_peak = jnp.max(peak, axis=0, keepdims=True)
            total = jnp.transpose(lanes[1, at, :]) * jnp.exp(peak - row_peak)
            rel_stats[0, p] = row_peak + jnp.log(jnp.sum(total, axis=0, keepdims=True))
            rel_stats[1, p] = jnp.sum(jnp.transpose(lanes[2, at, :]), axis=0, keepdims=True)

    lab_copies = []
    for m in range(1, n_v):
        copy = pltpu.make_async_remote_copy(
            src_ref=lab_ref, dst_ref=labs.at[pos[m]],
            send_sem=lab_send.at[m - 1], recv_sem=lab_recv.at[m - 1],
            device_id=(flip(v, m), z), device_id_type=MESH,
        )
        copy.start()
        lab_copies.append(copy)
    labs[0] = lab_ref[...]

    ops = plan(n_v // 2, n_h, cuts)
    tuned = [("cb"[kind - 2], g, s) if kind > 1 else ("sw"[kind], (g, s), cut) for kind, g, s, cut in ORDER]
    if sorted(map(str, ops)) == sorted(str(op) for op in tuned if op[0] != "b"):
        ops = tuned
    begin = 0
    while ops[begin][0] == "s":
        begin += 1
    for _, (g, s), cut in ops[:begin]:
        hand_on(0, 0, (g, s), parent(g, s)[1], cut)
    for cut in range(cuts):
        send(0, 0, 1, 0, cut, (flip(v, 1), z))
    units, prepared, known = [], [], set()
    for op in ops[begin:] + [None]:
        if op is not None and op[0] == "c":
            units.append(op[1:])
            continue
        if units:
            if not prepared and any(steps.get(g, 0) + sum(u[0] == g for u in units) == n_h for g, _ in units):
                prepare()
                prepared.append(True)
            multiply(units)
            for g, _ in units:
                if op is not None and steps[g] == n_h and g not in known:
                    known.add(g)
                    stats(groups_at[g], 1)
            units = []
        if op is None:
            break
        if op[0] == "b":
            continue
        if op[0] == "s":
            hand_on(0, 0, op[1], parent(*op[1])[1], op[2])
        else:
            arrive(*op[1], op[2])
    rest = [i for i, g in enumerate(groups) if g not in known]
    while rest:
        count = 1
        while count < len(rest) and rest[count] == rest[0] + count:
            count += 1
        stats(rest[0], count)
        rest = rest[count:]

    for m in range(n_v):
        for l in range(layers):
            for k in range(2):
                line[z, pl.ds(k * blocks + flip(v, m) * layers + l, 1), :] = rel_stats[k, pos[m] * layers + l]
    line_copies = []
    for j, peer in enumerate(line_peers):
        copy = pltpu.make_async_remote_copy(
            src_ref=line.at[z], dst_ref=line.at[z],
            send_sem=line_send.at[j], recv_sem=line_recv.at[j],
            device_id=(v, peer), device_id_type=MESH,
        )
        copy.start()
        line_copies.append(copy)
    for copy in line_copies:
        copy.wait_recv()
    whole, picked = combine([line[h] for h in range(n_h)], blocks)
    plane[v, 0:blocks, :] = whole
    plane[v, blocks : 2 * blocks, :] = picked
    plane_copies = []
    for m in range(1, n_v):
        copy = pltpu.make_async_remote_copy(
            src_ref=plane.at[v], dst_ref=plane.at[v],
            send_sem=plane_send.at[m - 1], recv_sem=plane_recv.at[m - 1],
            device_id=(flip(v, m), z), device_id_type=MESH,
        )
        copy.start()
        plane_copies.append(copy)
    for copy in sends + line_copies:
        copy.wait_send()
    for copy in plane_copies:
        copy.wait_recv()
    whole, picked = combine([plane[u] for u in range(n_v)], blocks)
    loss = whole - picked
    for l in range(layers):
        sums = jnp.zeros((1, LANES), jnp.float32)
        for u in range(n_v):
            row = loss[u * layers + l : u * layers + l + 1]
            loss_ref[l : l + 1, u * LANES : (u + 1) * LANES] = row
            sums = sums + row
        mean_ref[l] = jnp.sum(sums) / (n_v * LANES)
    for copy in plane_copies:
        copy.wait_send()


def body(hidden, unembed, labels, n_v, n_h):
    layers, tokens, depth = hidden.shape
    cols = unembed.shape[1]
    rows = layers * tokens
    blocks = n_v * layers
    dma = pltpu.SemaphoreType.DMA
    any_space = pl.BlockSpec(memory_space=pl.ANY)
    vmem = pl.BlockSpec(memory_space=pltpu.VMEM)
    cuts = CUTS if n_v * n_h <= 64 else 1
    return pl.pallas_call(
        functools.partial(kernel, n_v, n_h, layers),
        out_shape=(
            jax.ShapeDtypeStruct((layers, n_v * tokens), jnp.float32),
            jax.ShapeDtypeStruct((layers,), jnp.float32),
        ),
        in_specs=[any_space, any_space, vmem],
        out_specs=(vmem, pl.BlockSpec(memory_space=pltpu.SMEM)),
        scratch_shapes=[
            pltpu.VMEM((n_v * rows, n_h * depth), jnp.bfloat16),
            pltpu.VMEM((n_h * depth, cols), jnp.bfloat16),
            pltpu.VMEM((n_v * rows, cols), jnp.float32),
            pltpu.VMEM((n_v, 1, tokens), jnp.int32),
            pltpu.VMEM((4, n_v * rows, LANES), jnp.float32),
            pltpu.VMEM((2, blocks, 1, tokens), jnp.float32),
            pltpu.VMEM((n_h, 2 * blocks, tokens), jnp.float32),
            pltpu.VMEM((n_v, 2 * blocks, tokens), jnp.float32),
            dma,
            dma((n_h,)),
            dma(((n_v * n_h - 1) * cuts,)),
            dma((n_v * n_h * cuts,)),
            dma((n_v - 1,)),
            dma((n_v - 1,)),
            dma((n_h - 1,)),
            dma((n_h - 1,)),
            dma((n_v - 1,)),
            dma((n_v - 1,)),
        ],
        compiler_params=pltpu.CompilerParams(
            collective_id=0, has_side_effects=True, vmem_limit_bytes=60 * 2**20
        ),
    )(hidden.reshape(rows, depth), unembed, labels.reshape(1, tokens))


def solution(mesh):
    placed = (P(None, "vocab", "hid"), P(None, ("vocab", "hid")), P("vocab"))
    inner = functools.partial(body, n_v=mesh.shape["vocab"], n_h=mesh.shape["hid"])
    return jax.shard_map(inner, mesh=mesh, in_specs=placed, out_specs=(P(), P()), check_vma=False)
```
